128 devices in a mesh: space: 8 (over y_lo, z), tm: 16 (over y_hi, x, core).
Axes of the slice: x: 4, y: 4 (y_hi: 2, y_lo: 2; y = y_hi * 2 + y_lo), z: 4, core: 2. Of those that a mesh axis runs over, the one named last changes fastest.
Arguments:
- coefficients: float32 [2048, 8192], P('tm', 'space'), may hold values from -6 to 6
- counts: int32 [2048, 8192], P('tm', 'space'), may hold values from 0 to 2
- coords: float32 [2, 8192], replicated, may hold values from 0 to 12
- pattern: int32 [64, 8], replicated, may hold values from 0 to 63, as said below
- temporal_taps: float32 [9], replicated, may hold values from 0.05 to 0.35
Outputs:
- newton_step: float32 [2048, 8192], P('tm', 'space')
- residual: float32 [2048, 8192], P('tm', 'space')
The draws below stay inside these ranges and needn't reach their ends.
Inputs may be any that keep to these rules, and one draw needn't show every extreme that they name: `pattern`: each row lists 8 distinct block indices including the row's own index, and block j appears in row i exactly when block i appears in row j.
All inputs are finite; a program needn't handle non-finite values.
Results may differ from the reference program's by a relative error of at most 0.00016.
Values sent between devices are 32-bit elements; how exact they have to be, the bound alone decides.
A program may use at most 64 MiB of HBM per device.

```python
import math
import jax
import jax.numpy as jnp
from jax import lax

BLOCK = 128
NB = 8
BW = 8
ITERS = 2
NBLK = 64
CELLS = 8192
DAYS = 2048


strip_width = 0.125


strip_length = 8.0


def tile_layout(key):
    block_of = jax.random.permutation(jax.random.fold_in(key, 21), NBLK).astype(jnp.int32)
    places = jnp.arange(NBLK, dtype=jnp.int32)
    place_of = jnp.zeros((NBLK,), jnp.int32).at[block_of].set(places)
    return (block_of, place_of)


def draw_pattern(key, part):
    block_of, place_of = tile_layout(key)
    columns = NBLK // 2
    places = jnp.arange(NBLK, dtype=jnp.int32)
    column = places // 2
    cycle = places % 2
    step_col = jnp.array([0, 1, -1, 2, -2, 0, 1, -1], jnp.int32)
    step_cycle = jnp.array([0, 0, 0, 0, 0, 1, 1, 1], jnp.int32)
    near_col = (column[:, None] + step_col[None, :]) % columns
    near_cycle = (cycle[:, None] + step_cycle[None, :]) % 2
    near_place = near_col * 2 + near_cycle
    by_place = block_of[near_place]
    listed = jnp.zeros((NBLK, NB), jnp.int32).at[block_of].set(by_place)
    key_order = jax.random.fold_in(key, 13)
    orders = jax.vmap(lambda sub_key: jax.random.permutation(sub_key, NB))(jax.random.split(key_order, NBLK))
    return jnp.take_along_axis(listed, orders.astype(jnp.int32), axis=1)


def draw_coords(key, part):
    block_of, place_of = tile_layout(key)
    column = (place_of // 2).astype(jnp.float32)
    across = jax.random.uniform(jax.random.fold_in(key, 31), (NBLK, BLOCK), jnp.float32)
    along = jax.random.uniform(jax.random.fold_in(key, 32), (NBLK, BLOCK), jnp.float32)
    first = ((column[:, None] + across) * strip_width).reshape(CELLS)
    second = (along * strip_length).reshape(CELLS)
    return jnp.stack([first, second]).astype(jnp.float32)


def set_ends(entries, key, least, high):
    index_at = [jax.random.randint(jax.random.fold_in(key, axis), (), 0, length) for axis, length in enumerate(entries.shape)]
    widest = entries.shape.index(max(entries.shape))
    beside = index_at[:widest] + [(index_at[widest] + 1) % entries.shape[widest]] + index_at[widest + 1:]
    return entries.at[tuple(index_at)].set(least).at[tuple(beside)].set(high)


def level_of(rng, extent, shards, least, top_value):
    gain, own = 1.0, jax.random.fold_in(rng, 6)
    for position, shards_of in shards:
        draws = jnp.exp(jax.random.uniform(jax.random.fold_in(own, position), (shards_of,), jnp.float32, least / len(shards), top_value / len(shards)))
        gain = gain * jnp.repeat(draws, extent[position] // shards_of).reshape([-1 if axis == position else 1 for axis in range(len(extent))])
    return gain


def scatter_about(stream_key, extent, scale, reach, cuts=(), kind=jnp.bfloat16):
    level = level_of(stream_key, extent, cuts, -0.22, 0.18) if cuts else 1.0
    values = jax.random.normal(stream_key, extent, jnp.float32) * scale * level
    return jnp.minimum(jnp.maximum(values, -reach), reach).astype(kind)


def setup_inputs(seed: int = 0) -> dict:
    key_of = jax.random.split(jax.random.key(seed), 6)
    coefficients = scatter_about(key_of[0], (DAYS, CELLS), 1.0, 6.0, ((0, 16), (1, 8)), jnp.float32)
    counts = set_ends(jax.random.randint(key_of[1], (DAYS, CELLS), 0, 3), jax.random.fold_in(key_of[1], 1), 0, 2).astype(jnp.int32)
    coords = draw_coords(jax.random.fold_in(key_of[5], 71), 0)
    pattern = draw_pattern(jax.random.fold_in(key_of[5], 71), 0)
    temporal_taps = jnp.clip(jnp.exp(jax.random.uniform(key_of[4], (BW + 1,), jnp.float32, math.log(0.05), math.log(0.35))), 0.05, 0.35)
    return dict(coefficients=coefficients, counts=counts, coords=coords, pattern=pattern, temporal_taps=temporal_taps)


support = 0.25
amplitude = 0.2
row_group = 16

def wendland(distance):
    scaled = distance / support
    remain = jnp.maximum(1.0 - scaled, 0.0)
    return amplitude * remain ** 4 * (1.0 + 4.0 * scaled)

def band_product(field, temporal_taps):
    length = field.shape[0]
    padded = jnp.pad(field, ((BW, BW), (0, 0)))
    summed = temporal_taps[0] * field
    for offset in range(1, BW + 1):
        summed = summed + temporal_taps[offset] * (padded[BW - offset:BW - offset + length] + padded[BW + offset:BW + offset + length])
    return summed

def block_product(field, coords, pattern):
    day_count = field.shape[0]
    blocks = pattern.shape[0]
    blocked = field.reshape(day_count, blocks, BLOCK)
    located = coords.reshape(2, blocks, BLOCK)

    def group_out(first_row):
        row_ids = first_row + jnp.arange(row_group).astype(jnp.int32)
        columns = pattern[row_ids]
        row_coords = located[:, row_ids]
        col_coords = located[:, columns]
        delta_x = row_coords[0][:, None, :, None] - col_coords[0][:, :, None, :]
        delta_y = row_coords[1][:, None, :, None] - col_coords[1][:, :, None, :]
        weight = wendland(jnp.sqrt(delta_x * delta_x + delta_y * delta_y))
        picked = blocked[:, columns]
        return jnp.einsum('rjab,drjb->dra', weight, picked, precision=lax.Precision.HIGHEST)
    starts = (jnp.arange(blocks // row_group) * row_group).astype(jnp.int32)
    outputs = lax.map(group_out, starts)
    return outputs.transpose(1, 0, 2, 3).reshape(day_count, blocks * BLOCK)

def reference(coefficients, counts, coords, pattern, temporal_taps):

    def spread(field):
        return block_product(band_product(field, temporal_taps), coords, pattern)
    latent = spread(coefficients)
    intensity = jnp.exp(latent)
    gradient = coefficients + spread(intensity - counts.astype(jnp.float32))
    residual = -gradient
    direction = residual
    newton_step = jnp.zeros_like(residual)
    norm_now = jnp.sum(residual * residual)
    for iteration in range(ITERS):
        image = spread(direction)
        curved = direction + spread(intensity * image)
        step_size = norm_now / jnp.sum(direction * curved)
        newton_step = newton_step + step_size * direction
        residual = residual - step_size * curved
        if iteration + 1 < ITERS:
            norm_next = jnp.sum(residual * residual)
            direction = residual + norm_next / norm_now * direction
            norm_now = norm_next
    return (newton_step, residual)
```

```python
import jax
import jax.numpy as jnp
from jax import lax
from jax.sharding import PartitionSpec as P

BLOCK = 128
BW = 8
ITERS = 2


support = 0.25
amplitude = 0.2


def wendland(distance):
    scaled = distance / support
    remain = jnp.maximum(1.0 - scaled, 0.0)
    return amplitude * remain**4 * (1.0 + 4.0 * scaled)


def spatial_weights(coords, pattern):
    blocks = pattern.shape[0]
    located = coords.reshape(2, blocks, BLOCK)
    row_coords = located[:, :, None, None, :]
    col_coords = located[:, pattern][:, :, :, :, None]
    delta_x = row_coords[0] - col_coords[0]
    delta_y = row_coords[1] - col_coords[1]
    weight = wendland(jnp.sqrt(delta_x * delta_x + delta_y * delta_y))
    return weight.reshape(blocks, pattern.shape[1] * BLOCK, BLOCK)


def day_order_halo(field):
    spaces, times = lax.axis_size("space"), lax.axis_size("tm")
    place = [(rank % spaces) * times + rank // spaces for rank in range(spaces * times)]
    forward = [(place[i], place[i + 1]) for i in range(len(place) - 1)]
    backward = [(place[i + 1], place[i]) for i in range(len(place) - 1)]
    axes = ("space", "tm")
    low = lax.ppermute(field[field.shape[0] - BW :], axes, forward)
    high = lax.ppermute(field[:BW], axes, backward)
    return jnp.concatenate([low, field, high], axis=0)


def band_product(field, temporal_taps):
    length = field.shape[0]
    padded = day_order_halo(field)
    summed = temporal_taps[0] * field
    for offset in range(1, BW + 1):
        summed = summed + temporal_taps[offset] * (
            padded[BW - offset : BW - offset + length] + padded[BW + offset : BW + offset + length]
        )
    return summed


def block_product(field, weights, pattern):
    day_count = field.shape[0]
    blocks = pattern.shape[0]
    blocked = field.reshape(day_count, blocks, BLOCK)
    picked = blocked[:, pattern].reshape(day_count, blocks, pattern.shape[1] * BLOCK)
    out = jnp.einsum("rkc,drk->drc", weights, picked, precision=lax.Precision.HIGH)
    return out.reshape(day_count, blocks * BLOCK)


def to_days(field):
    return lax.all_to_all(field, "space", split_axis=1, concat_axis=2, tiled=True)


def to_cells(field):
    return lax.all_to_all(field, "space", split_axis=2, concat_axis=1, tiled=True)


def total(values):
    v = jnp.broadcast_to(jnp.stack(values)[:, None], (len(values), 128))
    for axis in ("space", "tm"):
        n = lax.axis_size(axis)
        k = 1
        while k < n:
            v = v + lax.ppermute(v, axis, [(i, i ^ k) for i in range(n)])
            k *= 2
    return [v[i, 0] for i in range(len(values))]


def shards(coefficients, counts, coords, pattern, temporal_taps):
    weights = spatial_weights(coords, pattern)

    def spread(field):
        return block_product(band_product(field, temporal_taps), weights, pattern)

    both = to_days(jnp.stack([coefficients, counts.astype(jnp.float32)]))
    coef, cnt = both[0], both[1]
    latent = spread(coef)
    intensity = jnp.exp(latent)
    gradient = coef + spread(intensity - cnt)
    residual = -gradient
    direction = residual
    newton_step = jnp.zeros_like(residual)
    norm_part = jnp.sum(residual * residual)
    norm_now = None
    for iteration in range(ITERS):
        image = spread(direction)
        weighted = intensity * image
        curv_part = jnp.sum(direction * direction) + jnp.sum(weighted * image)
        if norm_now is None:
            norm_now, curvature = total([norm_part, curv_part])
        else:
            (curvature,) = total([curv_part])
        curved = direction + spread(weighted)
        step_size = norm_now / curvature
        newton_step = newton_step + step_size * direction
        residual = residual - step_size * curved
        if iteration + 1 < ITERS:
            (norm_next,) = total([jnp.sum(residual * residual)])
            direction = residual + norm_next / norm_now * direction
            norm_now = norm_next
    out = to_cells(jnp.stack([newton_step, residual]))
    return (out[0], out[1])


def solution(mesh):
    placed = (P("tm", "space"), P("tm", "space"), P(), P(), P())
    return jax.shard_map(
        shards,
        mesh=mesh,
        in_specs=placed,
        out_specs=(P("tm", "space"), P("tm", "space")),
        check_vma=False,
    )
```

```python
import jax
import jax.numpy as jnp
from jax import lax
from jax.sharding import PartitionSpec as P

BLOCK = 128
BW = 8
ITERS = 2


support = 0.25
amplitude = 0.2


def wendland(distance):
    scaled = distance / support
    remain = jnp.maximum(1.0 - scaled, 0.0)
    return amplitude * remain**4 * (1.0 + 4.0 * scaled)


def spatial_weights(coords, pattern):
    blocks = pattern.shape[0]
    located = coords.reshape(2, blocks, BLOCK)
    row_coords = located[:, :, None, None, :]
    col_coords = located[:, pattern][:, :, :, :, None]
    delta_x = row_coords[0] - col_coords[0]
    delta_y = row_coords[1] - col_coords[1]
    weight = wendland(jnp.sqrt(delta_x * delta_x + delta_y * delta_y))
    return weight.reshape(blocks, pattern.shape[1] * BLOCK, BLOCK)


def day_order_halo(field):
    spaces, times = lax.axis_size("space"), lax.axis_size("tm")
    place = [(rank % spaces) * times + rank // spaces for rank in range(spaces * times)]
    forward = [(place[i], place[i + 1]) for i in range(len(place) - 1)]
    backward = [(place[i + 1], place[i]) for i in range(len(place) - 1)]
    axes = ("space", "tm")
    low = lax.ppermute(field[field.shape[0] - BW :], axes, forward)
    high = lax.ppermute(field[:BW], axes, backward)
    return jnp.concatenate([low, field, high], axis=0)


def band_product(field, temporal_taps):
    length = field.shape[0]
    padded = day_order_halo(field)
    summed = temporal_taps[0] * field
    for offset in range(1, BW + 1):
        summed = summed + temporal_taps[offset] * (
            padded[BW - offset : BW - offset + length] + padded[BW + offset : BW + offset + length]
        )
    return summed


def block_product(field, weights, pattern):
    day_count = field.shape[0]
    blocks = pattern.shape[0]
    blocked = field.reshape(day_count, blocks, BLOCK)
    picked = blocked[:, pattern].reshape(day_count, blocks, pattern.shape[1] * BLOCK)
    out = jnp.einsum("rkc,drk->drc", weights, picked, precision=lax.Precision.HIGH)
    return out.reshape(day_count, blocks * BLOCK)


def to_days(field):
    n = lax.axis_size("space")
    k, days, cells = field.shape
    chunked = field.reshape(k, n, days // n, cells).transpose(1, 0, 2, 3)
    got = lax.all_to_all(chunked, "space", split_axis=0, concat_axis=0, tiled=True)
    return got.transpose(1, 2, 0, 3).reshape(k, days // n, n * cells)


def to_cells(field):
    n = lax.axis_size("space")
    k, days, cells = field.shape
    chunked = field.reshape(k, days, n, cells // n).transpose(2, 0, 1, 3)
    got = lax.all_to_all(chunked, "space", split_axis=0, concat_axis=0, tiled=True)
    return got.transpose(1, 0, 2, 3).reshape(k, n * days, cells // n)


def total(values):
    v = jnp.broadcast_to(jnp.stack(values)[:, None], (len(values), 128))
    for axis in ("space", "tm"):
        n = lax.axis_size(axis)
        k = 1
        while k < n:
            v = v + lax.ppermute(v, axis, [(i, i ^ k) for i in range(n)])
            k *= 2
    return [v[i, 0] for i in range(len(values))]


def shards(coefficients, counts, coords, pattern, temporal_taps):
    weights = lax.optimization_barrier(spatial_weights(coords, pattern))

    def spread(field):
        return block_product(band_product(field, temporal_taps), weights, pattern)

    both = to_days(jnp.stack([coefficients, counts.astype(jnp.float32)]))
    coef, cnt = both[0], both[1]
    latent = spread(coef)
    intensity = jnp.exp(latent)
    gradient = coef + spread(intensity - cnt)
    residual = -gradient
    direction = residual
    newton_step = jnp.zeros_like(residual)
    norm_part = jnp.sum(residual * residual)
    norm_now = None
    for iteration in range(ITERS):
        image = spread(direction)
        weighted = intensity * image
        curv_part = jnp.sum(direction * direction) + jnp.sum(weighted * image)
        if norm_now is None:
            norm_now, curvature = total([norm_part, curv_part])
        else:
            (curvature,) = total([curv_part])
        curved = direction + spread(weighted)
        step_size = norm_now / curvature
        newton_step = newton_step + step_size * direction
        residual = residual - step_size * curved
        if iteration + 1 < ITERS:
            (norm_next,) = total([jnp.sum(residual * residual)])
            direction = residual + norm_next / norm_now * direction
            norm_now = norm_next
    out = to_cells(jnp.stack([newton_step, residual]))
    return (out[0], out[1])


def solution(mesh):
    placed = (P("tm", "space"), P("tm", "space"), P(), P(), P())
    return jax.shard_map(
        shards,
        mesh=mesh,
        in_specs=placed,
        out_specs=(P("tm", "space"), P("tm", "space")),
        check_vma=False,
    )
```

```python
import functools

import jax
import jax.numpy as jnp
from jax import lax
from jax.experimental import pallas as pl
from jax.experimental.pallas import tpu as pltpu
from jax.sharding import PartitionSpec as P

BLOCK = 128
BW = 8
ITERS = 2


support = 0.25
amplitude = 0.2


def wendland(distance):
    scaled = distance / support
    remain = jnp.maximum(1.0 - scaled, 0.0)
    return amplitude * remain**4 * (1.0 + 4.0 * scaled)


def spatial_weights(coords, pattern):
    blocks = pattern.shape[0]
    located = coords.reshape(2, blocks, BLOCK)
    row_coords = located[:, :, None, None, :]
    col_coords = located[:, pattern][:, :, :, :, None]
    delta_x = row_coords[0] - col_coords[0]
    delta_y = row_coords[1] - col_coords[1]
    weight = wendland(jnp.sqrt(delta_x * delta_x + delta_y * delta_y))
    return weight.reshape(blocks, pattern.shape[1] * BLOCK, BLOCK)


def day_order_halo(field):
    spaces, times = lax.axis_size("space"), lax.axis_size("tm")
    place = [(rank % spaces) * times + rank // spaces for rank in range(spaces * times)]
    forward = [(place[i], place[i + 1]) for i in range(len(place) - 1)]
    backward = [(place[i + 1], place[i]) for i in range(len(place) - 1)]
    axes = ("space", "tm")
    low = lax.ppermute(field[field.shape[0] - BW :], axes, forward)
    high = lax.ppermute(field[:BW], axes, backward)
    return jnp.concatenate([low, field, high], axis=0)


def band_product(field, temporal_taps):
    length = field.shape[0]
    padded = day_order_halo(field)
    summed = temporal_taps[0] * field
    for offset in range(1, BW + 1):
        summed = summed + temporal_taps[offset] * (
            padded[BW - offset : BW - offset + length] + padded[BW + offset : BW + offset + length]
        )
    return summed


def block_product(field, weights, pattern):
    day_count = field.shape[0]
    blocks = pattern.shape[0]
    blocked = field.reshape(day_count, blocks, BLOCK)
    picked = blocked[:, pattern].reshape(day_count, blocks, pattern.shape[1] * BLOCK)
    out = jnp.einsum("rkc,drk->drc", weights, picked, precision=lax.Precision.HIGH)
    return out.reshape(day_count, blocks * BLOCK)


def to_days(field):
    n = lax.axis_size("space")
    k, days, cells = field.shape
    chunked = field.reshape(k, n, days // n, cells).transpose(1, 0, 2, 3)
    got = lax.all_to_all(chunked, "space", split_axis=0, concat_axis=0, tiled=True)
    return got.transpose(1, 2, 0, 3).reshape(k, days // n, n * cells)


def to_cells(field):
    n = lax.axis_size("space")
    k, days, cells = field.shape
    chunked = field.reshape(k, days, n, cells // n).transpose(2, 0, 1, 3)
    got = lax.all_to_all(chunked, "space", split_axis=0, concat_axis=0, tiled=True)
    return got.transpose(1, 0, 2, 3).reshape(k, n * days, cells // n)


def group_sum_kernel(axis, x_ref, o_ref, slots, send, recv):
    n = slots.shape[0]
    me = lax.axis_index(axis)

    def peer(index):
        return {axis: index}

    barrier = pltpu.get_barrier_semaphore()
    for k in range(1, n):
        pl.semaphore_signal(barrier, 1, device_id=peer(lax.rem(me + k, n)), device_id_type=pl.DeviceIdType.MESH)
    pl.semaphore_wait(barrier, n - 1)
    copies = []
    for k in range(1, n):
        target = lax.rem(me + k, n)
        copy = pltpu.make_async_remote_copy(
            src_ref=x_ref,
            dst_ref=slots.at[me],
            send_sem=send.at[target],
            recv_sem=recv.at[me],
            device_id=peer(target),
            device_id_type=pl.DeviceIdType.MESH,
        )
        copy.start()
        copies.append(copy)
    slots[me] = x_ref[...]
    for k in range(1, n):
        source = lax.rem(me - k + n, n)
        pltpu.make_async_remote_copy(
            src_ref=x_ref,
            dst_ref=slots.at[source],
            send_sem=send.at[source],
            recv_sem=recv.at[source],
            device_id=peer(source),
            device_id_type=pl.DeviceIdType.MESH,
        ).wait_recv()
    for copy in copies:
        copy.wait_send()
    acc = slots[0]
    for j in range(1, n):
        acc = acc + slots[j]
    o_ref[...] = acc


def group_sum(tile, axis, collective_id):
    n = lax.axis_size(axis)
    return pl.pallas_call(
        functools.partial(group_sum_kernel, axis),
        out_shape=jax.ShapeDtypeStruct(tile.shape, tile.dtype),
        in_specs=[pl.BlockSpec(memory_space=pltpu.VMEM)],
        out_specs=pl.BlockSpec(memory_space=pltpu.VMEM),
        scratch_shapes=[
            pltpu.VMEM((n,) + tile.shape, tile.dtype),
            pltpu.SemaphoreType.DMA((n,)),
            pltpu.SemaphoreType.DMA((n,)),
        ],
        compiler_params=pltpu.CompilerParams(collective_id=collective_id, has_side_effects=True),
    )(tile)


def total(values):
    tile = jnp.zeros((8, 128), jnp.float32) + jnp.stack(values + [values[0]] * (8 - len(values)))[:, None]
    tile = group_sum(group_sum(tile, "space", 0), "tm", 1)
    return [tile[i, 0] for i in range(len(values))]


def shards(coefficients, counts, coords, pattern, temporal_taps):
    weights = lax.optimization_barrier(spatial_weights(coords, pattern))

    def spread(field):
        return block_product(band_product(field, temporal_taps), weights, pattern)

    both = to_days(jnp.stack([coefficients, counts.astype(jnp.float32)]))
    coef, cnt = both[0], both[1]
    latent = spread(coef)
    intensity = jnp.exp(latent)
    gradient = coef + spread(intensity - cnt)
    residual = -gradient
    direction = residual
    newton_step = jnp.zeros_like(residual)
    norm_part = jnp.sum(residual * residual)
    norm_now = None
    for iteration in range(ITERS):
        image = spread(direction)
        weighted = intensity * image
        curv_part = jnp.sum(direction * direction) + jnp.sum(weighted * image)
        if norm_now is None:
            norm_now, curvature = total([norm_part, curv_part])
        else:
            (curvature,) = total([curv_part])
        curved = direction + spread(weighted)
        step_size = norm_now / curvature
        newton_step = newton_step + step_size * direction
        residual = residual - step_size * curved
        if iteration + 1 < ITERS:
            (norm_next,) = total([jnp.sum(residual * residual)])
            direction = residual + norm_next / norm_now * direction
            norm_now = norm_next
    out = to_cells(jnp.stack([newton_step, residual]))
    return (out[0], out[1])


def solution(mesh):
    placed = (P("tm", "space"), P("tm", "space"), P(), P(), P())
    return jax.shard_map(
        shards,
        mesh=mesh,
        in_specs=placed,
        out_specs=(P("tm", "space"), P("tm", "space")),
        check_vma=False,
    )
```

```python
import functools

import jax
import jax.numpy as jnp
from jax import lax
from jax.experimental import pallas as pl
from jax.experimental.pallas import tpu as pltpu
from jax.sharding import PartitionSpec as P

BLOCK = 128
BW = 8


support = 0.25
amplitude = 0.2


def wendland(distance):
    scaled = distance / support
    remain = jnp.maximum(1.0 - scaled, 0.0)
    return amplitude * remain**4 * (1.0 + 4.0 * scaled)


def spatial_weights(coords, pattern):
    blocks = pattern.shape[0]
    located = coords.reshape(2, blocks, BLOCK)
    row_coords = located[:, :, None, None, :]
    col_coords = located[:, pattern][:, :, :, :, None]
    delta_x = row_coords[0] - col_coords[0]
    delta_y = row_coords[1] - col_coords[1]
    weight = wendland(jnp.sqrt(delta_x * delta_x + delta_y * delta_y))
    return weight.reshape(blocks, pattern.shape[1] * BLOCK, BLOCK)


def day_order_halo(field):
    spaces, times = lax.axis_size("space"), lax.axis_size("tm")
    place = [(rank % spaces) * times + rank // spaces for rank in range(spaces * times)]
    forward = [(place[i], place[i + 1]) for i in range(len(place) - 1)]
    backward = [(place[i + 1], place[i]) for i in range(len(place) - 1)]
    axes = ("space", "tm")
    low = lax.ppermute(field[field.shape[0] - BW :], axes, forward)
    high = lax.ppermute(field[:BW], axes, backward)
    return jnp.concatenate([low, field, high], axis=0)


def tm_halo(field):
    count = lax.axis_size("tm")
    forward = [(i, i + 1) for i in range(count - 1)]
    backward = [(i + 1, i) for i in range(count - 1)]
    low = lax.ppermute(field[field.shape[0] - BW :], "tm", forward)
    high = lax.ppermute(field[:BW], "tm", backward)
    return jnp.concatenate([low, field, high], axis=0)


def band_product(field, temporal_taps, halo=None):
    length = field.shape[0]
    padded = (halo or day_order_halo)(field)
    summed = temporal_taps[0] * field
    for offset in range(1, BW + 1):
        summed = summed + temporal_taps[offset] * (
            padded[BW - offset : BW - offset + length] + padded[BW + offset : BW + offset + length]
        )
    return summed


def block_product(field, weights, pattern):
    day_count = field.shape[0]
    blocks = pattern.shape[0]
    blocked = field.reshape(day_count, blocks, BLOCK)
    picked = blocked[:, pattern].reshape(day_count, blocks, pattern.shape[1] * BLOCK)
    out = jnp.einsum("rkc,drk->drc", weights, picked, precision=lax.Precision.HIGH)
    return out.reshape(day_count, blocks * BLOCK)


def to_days(field):
    n = lax.axis_size("space")
    k, days, cells = field.shape
    chunked = field.reshape(k, n, days // n, cells).transpose(1, 0, 2, 3)
    got = lax.all_to_all(chunked, "space", split_axis=0, concat_axis=0, tiled=True)
    return got.transpose(1, 2, 0, 3).reshape(k, days // n, n * cells)


def to_cells(field):
    n = lax.axis_size("space")
    k, days, cells = field.shape
    chunked = field.reshape(k, days, n, cells // n).transpose(2, 0, 1, 3)
    got = lax.all_to_all(chunked, "space", split_axis=0, concat_axis=0, tiled=True)
    return got.transpose(1, 0, 2, 3).reshape(k, n * days, cells // n)


def group_sum_kernel(axis, x_ref, o_ref, slots, send, recv):
    n = slots.shape[0]
    me = lax.axis_index(axis)

    def peer(index):
        return {axis: index}

    barrier = pltpu.get_barrier_semaphore()
    for k in range(1, n):
        pl.semaphore_signal(barrier, 1, device_id=peer(lax.rem(me + k, n)), device_id_type=pl.DeviceIdType.MESH)
    pl.semaphore_wait(barrier, n - 1)
    copies = []
    for k in range(1, n):
        target = lax.rem(me + k, n)
        copy = pltpu.make_async_remote_copy(
            src_ref=x_ref,
            dst_ref=slots.at[me],
            send_sem=send.at[target],
            recv_sem=recv.at[me],
            device_id=peer(target),
            device_id_type=pl.DeviceIdType.MESH,
        )
        copy.start()
        copies.append(copy)
    slots[me] = x_ref[...]
    for k in range(1, n):
        source = lax.rem(me - k + n, n)
        pltpu.make_async_remote_copy(
            src_ref=x_ref,
            dst_ref=slots.at[source],
            send_sem=send.at[source],
            recv_sem=recv.at[source],
            device_id=peer(source),
            device_id_type=pl.DeviceIdType.MESH,
        ).wait_recv()
    for copy in copies:
        copy.wait_send()
    acc = slots[0]
    for j in range(1, n):
        acc = acc + slots[j]
    o_ref[...] = acc


def group_sum(tile, axis, collective_id):
    n = lax.axis_size(axis)
    return pl.pallas_call(
        functools.partial(group_sum_kernel, axis),
        out_shape=jax.ShapeDtypeStruct(tile.shape, tile.dtype),
        in_specs=[pl.BlockSpec(memory_space=pltpu.VMEM)],
        out_specs=pl.BlockSpec(memory_space=pltpu.VMEM),
        scratch_shapes=[
            pltpu.VMEM((n,) + tile.shape, tile.dtype),
            pltpu.SemaphoreType.DMA((n,)),
            pltpu.SemaphoreType.DMA((n,)),
        ],
        compiler_params=pltpu.CompilerParams(collective_id=collective_id, has_side_effects=True),
    )(tile)


def total(values):
    tile = jnp.zeros((8, 128), jnp.float32) + jnp.stack(values + [values[0]] * (8 - len(values)))[:, None]
    tile = group_sum(group_sum(tile, "space", 0), "tm", 1)
    return [tile[i, 0] for i in range(len(values))]


def shards(coefficients, counts, coords, pattern, temporal_taps):
    weights = lax.optimization_barrier(spatial_weights(coords, pattern))

    def spread(field):
        return block_product(band_product(field, temporal_taps), weights, pattern)

    banded = band_product(coefficients, temporal_taps, tm_halo)
    moved = to_days(jnp.stack([coefficients, counts.astype(jnp.float32), banded]))
    coef, cnt = moved[0], moved[1]
    latent = block_product(moved[2], weights, pattern)
    intensity = jnp.exp(latent)
    gradient = coef + spread(intensity - cnt)
    residual = -gradient
    direction = residual
    image = spread(direction)
    curved = direction + spread(intensity * image)
    norm_now, curvature, curved_sq = total(
        [jnp.sum(residual * residual), jnp.sum(direction * curved), jnp.sum(curved * curved)]
    )
    step_size = norm_now / curvature
    newton_step = step_size * direction
    residual = residual - step_size * curved
    norm_next = step_size * step_size * curved_sq - norm_now
    direction = residual + norm_next / norm_now * direction
    norm_now = norm_next
    image = spread(direction)
    curved = direction + spread(intensity * image)
    (curvature,) = total([jnp.sum(direction * curved)])
    step_size = norm_now / curvature
    newton_step = newton_step + step_size * direction
    residual = residual - step_size * curved
    out = to_cells(jnp.stack([newton_step, residual]))
    return (out[0], out[1])


def solution(mesh):
    placed = (P("tm", "space"), P("tm", "space"), P(), P(), P())
    return jax.shard_map(
        shards,
        mesh=mesh,
        in_specs=placed,
        out_specs=(P("tm", "space"), P("tm", "space")),
        check_vma=False,
    )
```

```python
import functools

import jax
import jax.numpy as jnp
from jax import lax
from jax.experimental import pallas as pl
from jax.experimental.pallas import tpu as pltpu
from jax.sharding import PartitionSpec as P

BLOCK = 128
BW = 8


support = 0.25
amplitude = 0.2


def wendland(distance):
    scaled = distance / support
    remain = jnp.maximum(1.0 - scaled, 0.0)
    return amplitude * remain**4 * (1.0 + 4.0 * scaled)


def spatial_weights(coords, pattern):
    blocks = pattern.shape[0]
    located = coords.reshape(2, blocks, BLOCK)
    row_coords = located[:, :, None, None, :]
    col_coords = located[:, pattern][:, :, :, :, None]
    delta_x = row_coords[0] - col_coords[0]
    delta_y = row_coords[1] - col_coords[1]
    weight = wendland(jnp.sqrt(delta_x * delta_x + delta_y * delta_y))
    return weight.reshape(blocks, pattern.shape[1] * BLOCK, BLOCK)


def day_order_halo(field):
    spaces, times = lax.axis_size("space"), lax.axis_size("tm")
    place = [(rank % spaces) * times + rank // spaces for rank in range(spaces * times)]
    forward = [(place[i], place[i + 1]) for i in range(len(place) - 1)]
    backward = [(place[i + 1], place[i]) for i in range(len(place) - 1)]
    axes = ("space", "tm")
    low = lax.ppermute(field[field.shape[0] - BW :], axes, forward)
    high = lax.ppermute(field[:BW], axes, backward)
    return jnp.concatenate([low, field, high], axis=0)


def tm_halo(field):
    count = lax.axis_size("tm")
    forward = [(i, i + 1) for i in range(count - 1)]
    backward = [(i + 1, i) for i in range(count - 1)]
    low = lax.ppermute(field[field.shape[0] - BW :], "tm", forward)
    high = lax.ppermute(field[:BW], "tm", backward)
    return jnp.concatenate([low, field, high], axis=0)


def band_product(field, temporal_taps, halo=None):
    length = field.shape[0]
    padded = (halo or day_order_halo)(field)
    summed = temporal_taps[0] * field
    for offset in range(1, BW + 1):
        summed = summed + temporal_taps[offset] * (
            padded[BW - offset : BW - offset + length] + padded[BW + offset : BW + offset + length]
        )
    return summed


def block_product(field, weights, pattern):
    day_count = field.shape[0]
    blocks = pattern.shape[0]
    blocked = field.reshape(day_count, blocks, BLOCK)
    picked = blocked[:, pattern].reshape(day_count, blocks, pattern.shape[1] * BLOCK)
    out = jnp.einsum("rkc,drk->drc", weights, picked, precision=lax.Precision.HIGH)
    return out.reshape(day_count, blocks * BLOCK)


def to_days(field):
    n = lax.axis_size("space")
    k, days, cells = field.shape
    chunked = field.reshape(k, n, days // n, cells).transpose(1, 0, 2, 3)
    got = lax.all_to_all(chunked, "space", split_axis=0, concat_axis=0, tiled=True)
    return got.transpose(1, 2, 0, 3).reshape(k, days // n, n * cells)


def to_cells(field):
    n = lax.axis_size("space")
    k, days, cells = field.shape
    chunked = field.reshape(k, days, n, cells // n).transpose(2, 0, 1, 3)
    got = lax.all_to_all(chunked, "space", split_axis=0, concat_axis=0, tiled=True)
    return got.transpose(1, 0, 2, 3).reshape(k, n * days, cells // n)


def group_sum_kernel(axis, x_ref, o_ref, slots, send, recv):
    n = slots.shape[0]
    me = lax.axis_index(axis)

    def peer(index):
        return {axis: index}

    barrier = pltpu.get_barrier_semaphore()
    for k in range(1, n):
        pl.semaphore_signal(barrier, 1, device_id=peer(lax.rem(me + k, n)), device_id_type=pl.DeviceIdType.MESH)
    pl.semaphore_wait(barrier, n - 1)
    copies = []
    for k in range(1, n):
        target = lax.rem(me + k, n)
        copy = pltpu.make_async_remote_copy(
            src_ref=x_ref,
            dst_ref=slots.at[me],
            send_sem=send.at[target],
            recv_sem=recv.at[me],
            device_id=peer(target),
            device_id_type=pl.DeviceIdType.MESH,
        )
        copy.start()
        copies.append(copy)
    slots[me] = x_ref[...]
    for k in range(1, n):
        source = lax.rem(me - k + n, n)
        pltpu.make_async_remote_copy(
            src_ref=x_ref,
            dst_ref=slots.at[source],
            send_sem=send.at[source],
            recv_sem=recv.at[source],
            device_id=peer(source),
            device_id_type=pl.DeviceIdType.MESH,
        ).wait_recv()
    for copy in copies:
        copy.wait_send()
    acc = slots[0]
    for j in range(1, n):
        acc = acc + slots[j]
    o_ref[...] = acc


def group_sum(tile, axis, collective_id):
    n = lax.axis_size(axis)
    return pl.pallas_call(
        functools.partial(group_sum_kernel, axis),
        out_shape=jax.ShapeDtypeStruct(tile.shape, tile.dtype),
        in_specs=[pl.BlockSpec(memory_space=pltpu.VMEM)],
        out_specs=pl.BlockSpec(memory_space=pltpu.VMEM),
        scratch_shapes=[
            pltpu.VMEM((n,) + tile.shape, tile.dtype),
            pltpu.SemaphoreType.DMA((n,)),
            pltpu.SemaphoreType.DMA((n,)),
        ],
        compiler_params=pltpu.CompilerParams(collective_id=collective_id, has_side_effects=True),
    )(tile)


def total(values):
    tile = jnp.zeros((8, 128), jnp.float32) + jnp.stack(values + [values[0]] * (8 - len(values)))[:, None]
    tile = group_sum(group_sum(tile, "space", 0), "tm", 1)
    return [tile[i, 0] for i in range(len(values))]


def shards(coefficients, counts, coords, pattern, temporal_taps):
    weights = lax.optimization_barrier(spatial_weights(coords, pattern))

    def spread(field):
        return block_product(band_product(field, temporal_taps), weights, pattern)

    banded = band_product(coefficients, temporal_taps, tm_halo)
    moved = to_days(jnp.stack([coefficients, counts.astype(jnp.float32), banded]))
    coef, cnt = moved[0], moved[1]
    latent = block_product(moved[2], weights, pattern)
    intensity = jnp.exp(latent)
    gradient = coef + spread(intensity - cnt)
    residual = -gradient
    direction = residual
    image = spread(direction)
    curved = direction + spread(intensity * image)
    norm_now, curvature, curved_sq = total(
        [jnp.sum(residual * residual), jnp.sum(direction * curved), jnp.sum(curved * curved)]
    )
    step_size = norm_now / curvature
    newton_step = step_size * direction
    residual = residual - step_size * curved
    norm_next = step_size * step_size * curved_sq - norm_now
    direction = residual + norm_next / norm_now * direction
    norm_now = norm_next
    early = to_cells(jnp.stack([newton_step, direction, residual]))
    image = spread(direction)
    curved = direction + spread(intensity * image)
    late = to_cells(curved[None])
    (curvature,) = total([jnp.sum(direction * curved)])
    step_size = norm_now / curvature
    newton_step = early[0] + step_size * early[1]
    residual = early[2] - step_size * late[0]
    return (newton_step, residual)


def solution(mesh):
    placed = (P("tm", "space"), P("tm", "space"), P(), P(), P())
    return jax.shard_map(
        shards,
        mesh=mesh,
        in_specs=placed,
        out_specs=(P("tm", "space"), P("tm", "space")),
        check_vma=False,
    )
```

```python
import functools

import jax
import jax.numpy as jnp
from jax import lax
from jax.experimental import pallas as pl
from jax.experimental.pallas import tpu as pltpu
from jax.sharding import PartitionSpec as P

BLOCK = 128
BW = 8


support = 0.25
amplitude = 0.2


def wendland(distance):
    scaled = distance / support
    remain = jnp.maximum(1.0 - scaled, 0.0)
    return amplitude * remain**4 * (1.0 + 4.0 * scaled)


def spatial_weights(coords, pattern):
    blocks = pattern.shape[0]
    located = coords.reshape(2, blocks, BLOCK)
    row_coords = located[:, :, None, None, :]
    col_coords = located[:, pattern][:, :, :, :, None]
    delta_x = row_coords[0] - col_coords[0]
    delta_y = row_coords[1] - col_coords[1]
    weight = wendland(jnp.sqrt(delta_x * delta_x + delta_y * delta_y))
    return weight.reshape(blocks, pattern.shape[1] * BLOCK, BLOCK)


def day_order_halo(field):
    spaces, times = lax.axis_size("space"), lax.axis_size("tm")
    place = [(rank % spaces) * times + rank // spaces for rank in range(spaces * times)]
    forward = [(place[i], place[i + 1]) for i in range(len(place) - 1)]
    backward = [(place[i + 1], place[i]) for i in range(len(place) - 1)]
    axes = ("space", "tm")
    low = lax.ppermute(field[field.shape[0] - BW :], axes, forward)
    high = lax.ppermute(field[:BW], axes, backward)
    return jnp.concatenate([low, field, high], axis=0)


def tm_halo(field):
    count = lax.axis_size("tm")
    forward = [(i, i + 1) for i in range(count - 1)]
    backward = [(i + 1, i) for i in range(count - 1)]
    low = lax.ppermute(field[field.shape[0] - BW :], "tm", forward)
    high = lax.ppermute(field[:BW], "tm", backward)
    return jnp.concatenate([low, field, high], axis=0)


def band_product(field, temporal_taps, halo=None):
    length = field.shape[0]
    padded = (halo or day_order_halo)(field)
    summed = temporal_taps[0] * field
    for offset in range(1, BW + 1):
        summed = summed + temporal_taps[offset] * (
            padded[BW - offset : BW - offset + length] + padded[BW + offset : BW + offset + length]
        )
    return summed


def block_product(field, weights, pattern):
    day_count = field.shape[0]
    blocks = pattern.shape[0]
    blocked = field.reshape(day_count, blocks, BLOCK)
    picked = blocked[:, pattern].reshape(day_count, blocks, pattern.shape[1] * BLOCK)
    out = jnp.einsum("rkc,drk->drc", weights, picked, precision=lax.Precision.HIGH)
    return out.reshape(day_count, blocks * BLOCK)


def to_days(field):
    n = lax.axis_size("space")
    k, days, cells = field.shape
    chunked = field.reshape(k, n, days // n, cells).transpose(1, 0, 2, 3)
    got = lax.all_to_all(chunked, "space", split_axis=0, concat_axis=0, tiled=True)
    return got.transpose(1, 2, 0, 3).reshape(k, days // n, n * cells)


def to_cells(field):
    n = lax.axis_size("space")
    k, days, cells = field.shape
    chunked = field.reshape(k, days, n, cells // n).transpose(2, 0, 1, 3)
    got = lax.all_to_all(chunked, "space", split_axis=0, concat_axis=0, tiled=True)
    return got.transpose(1, 0, 2, 3).reshape(k, n * days, cells // n)


def all_sum_kernel(times, x_ref, o_ref, slots, send, recv):
    n = slots.shape[0]
    me = lax.axis_index("space") * times + lax.axis_index("tm")

    def peer(index):
        return (lax.div(index, times), lax.rem(index, times))

    def copy_with(slot, target):
        return pltpu.make_async_remote_copy(
            src_ref=x_ref,
            dst_ref=slots.at[slot],
            send_sem=send.at[target],
            recv_sem=recv.at[slot],
            device_id=peer(target),
            device_id_type=pl.DeviceIdType.MESH,
        )

    barrier = pltpu.get_barrier_semaphore()

    @pl.loop(1, n)
    def _(k):
        pl.semaphore_signal(barrier, 1, device_id=peer(lax.rem(me + k, n)), device_id_type=pl.DeviceIdType.MESH)

    pl.semaphore_wait(barrier, n - 1)

    @pl.loop(1, n)
    def _(k):
        copy_with(me, lax.rem(me + k, n)).start()

    slots[me] = x_ref[...]

    @pl.loop(1, n)
    def _(k):
        source = lax.rem(me - k + n, n)
        copy_with(source, source).wait_recv()

    @pl.loop(1, n)
    def _(k):
        copy_with(me, lax.rem(me + k, n)).wait_send()

    acc = slots[0]
    for j in range(1, n):
        acc = acc + slots[j]
    o_ref[...] = acc


def total(values):
    spaces, times = lax.axis_size("space"), lax.axis_size("tm")
    tile = jnp.zeros((8, 128), jnp.float32) + jnp.stack(values + [values[0]] * (8 - len(values)))[:, None]
    summed = pl.pallas_call(
        functools.partial(all_sum_kernel, times),
        out_shape=jax.ShapeDtypeStruct(tile.shape, tile.dtype),
        in_specs=[pl.BlockSpec(memory_space=pltpu.VMEM)],
        out_specs=pl.BlockSpec(memory_space=pltpu.VMEM),
        scratch_shapes=[
            pltpu.VMEM((spaces * times,) + tile.shape, tile.dtype),
            pltpu.SemaphoreType.DMA((spaces * times,)),
            pltpu.SemaphoreType.DMA((spaces * times,)),
        ],
        compiler_params=pltpu.CompilerParams(collective_id=0, has_side_effects=True),
    )(tile)
    return [summed[i, 0] for i in range(len(values))]


def shards(coefficients, counts, coords, pattern, temporal_taps):
    weights = lax.optimization_barrier(spatial_weights(coords, pattern))

    def spread(field):
        return block_product(band_product(field, temporal_taps), weights, pattern)

    banded = band_product(coefficients, temporal_taps, tm_halo)
    moved = to_days(jnp.stack([coefficients, counts.astype(jnp.float32), banded]))
    coef, cnt = moved[0], moved[1]
    latent = block_product(moved[2], weights, pattern)
    intensity = jnp.exp(latent)
    gradient = coef + spread(intensity - cnt)
    residual = -gradient
    direction = residual
    image = spread(direction)
    curved = direction + spread(intensity * image)
    norm_now, curvature, curved_sq = total(
        [jnp.sum(residual * residual), jnp.sum(direction * curved), jnp.sum(curved * curved)]
    )
    step_size = norm_now / curvature
    newton_step = step_size * direction
    residual = residual - step_size * curved
    norm_next = step_size * step_size * curved_sq - norm_now
    direction = residual + norm_next / norm_now * direction
    norm_now = norm_next
    image = spread(direction)
    curved = direction + spread(intensity * image)
    (curvature,) = total([jnp.sum(direction * curved)])
    step_size = norm_now / curvature
    newton_step = newton_step + step_size * direction
    residual = residual - step_size * curved
    out = to_cells(jnp.stack([newton_step, residual]))
    return (out[0], out[1])


def solution(mesh):
    placed = (P("tm", "space"), P("tm", "space"), P(), P(), P())
    return jax.shard_map(
        shards,
        mesh=mesh,
        in_specs=placed,
        out_specs=(P("tm", "space"), P("tm", "space")),
        check_vma=False,
    )
```

```python
import functools

import jax
import jax.numpy as jnp
from jax import lax
from jax.experimental import pallas as pl
from jax.experimental.pallas import tpu as pltpu
from jax.sharding import PartitionSpec as P

BLOCK = 128
BW = 8


support = 0.25
amplitude = 0.2


def wendland(distance):
    scaled = distance / support
    remain = jnp.maximum(1.0 - scaled, 0.0)
    return amplitude * remain**4 * (1.0 + 4.0 * scaled)


def spatial_weights(coords, pattern):
    blocks = pattern.shape[0]
    located = coords.reshape(2, blocks, BLOCK)
    row_coords = located[:, :, None, None, :]
    col_coords = located[:, pattern][:, :, :, :, None]
    delta_x = row_coords[0] - col_coords[0]
    delta_y = row_coords[1] - col_coords[1]
    weight = wendland(jnp.sqrt(delta_x * delta_x + delta_y * delta_y))
    return weight.reshape(blocks, pattern.shape[1] * BLOCK, BLOCK)


def day_order_halo(field):
    spaces, times = lax.axis_size("space"), lax.axis_size("tm")
    order = snake(spaces)
    place = [order[rank % spaces] * times + rank // spaces for rank in range(spaces * times)]
    forward = [(place[i], place[i + 1]) for i in range(len(place) - 1)]
    backward = [(place[i + 1], place[i]) for i in range(len(place) - 1)]
    axes = ("space", "tm")
    low = lax.ppermute(field[field.shape[0] - BW :], axes, forward)
    high = lax.ppermute(field[:BW], axes, backward)
    return jnp.concatenate([low, field, high], axis=0)


def tm_halo(field):
    count = lax.axis_size("tm")
    forward = [(i, i + 1) for i in range(count - 1)]
    backward = [(i + 1, i) for i in range(count - 1)]
    low = lax.ppermute(field[field.shape[0] - BW :], "tm", forward)
    high = lax.ppermute(field[:BW], "tm", backward)
    return jnp.concatenate([low, field, high], axis=0)


def band_product(field, temporal_taps, halo=None):
    length = field.shape[0]
    padded = (halo or day_order_halo)(field)
    summed = temporal_taps[0] * field
    for offset in range(1, BW + 1):
        summed = summed + temporal_taps[offset] * (
            padded[BW - offset : BW - offset + length] + padded[BW + offset : BW + offset + length]
        )
    return summed


def block_product(field, weights, pattern):
    day_count = field.shape[0]
    blocks = pattern.shape[0]
    blocked = field.reshape(day_count, blocks, BLOCK)
    picked = blocked[:, pattern].reshape(day_count, blocks, pattern.shape[1] * BLOCK)
    out = jnp.einsum("rkc,drk->drc", weights, picked, precision=lax.Precision.HIGH)
    return out.reshape(day_count, blocks * BLOCK)


def snake(spaces):
    half = spaces // 2
    return [i if i < half else spaces + half - 1 - i for i in range(spaces)]


def to_days(field):
    n = lax.axis_size("space")
    k, days, cells = field.shape
    chunked = field.reshape(k, n, days // n, cells)[:, jnp.array(snake(n))].transpose(1, 0, 2, 3)
    got = lax.all_to_all(chunked, "space", split_axis=0, concat_axis=0, tiled=True)
    return got.transpose(1, 2, 0, 3).reshape(k, days // n, n * cells)


def to_cells(field):
    n = lax.axis_size("space")
    k, days, cells = field.shape
    chunked = field.reshape(k, days, n, cells // n).transpose(2, 0, 1, 3)
    got = lax.all_to_all(chunked, "space", split_axis=0, concat_axis=0, tiled=True)
    return got[jnp.array(snake(n))].transpose(1, 0, 2, 3).reshape(k, n * days, cells // n)


def group_sum_kernel(axis, x_ref, o_ref, slots, send, recv):
    n = slots.shape[0]
    me = lax.axis_index(axis)

    def peer(index):
        return {axis: index}

    barrier = pltpu.get_barrier_semaphore()
    for k in range(1, n):
        pl.semaphore_signal(barrier, 1, device_id=peer(lax.rem(me + k, n)), device_id_type=pl.DeviceIdType.MESH)
    pl.semaphore_wait(barrier, n - 1)
    copies = []
    for k in range(1, n):
        target = lax.rem(me + k, n)
        copy = pltpu.make_async_remote_copy(
            src_ref=x_ref,
            dst_ref=slots.at[me],
            send_sem=send.at[target],
            recv_sem=recv.at[me],
            device_id=peer(target),
            device_id_type=pl.DeviceIdType.MESH,
        )
        copy.start()
        copies.append(copy)
    slots[me] = x_ref[...]
    for k in range(1, n):
        source = lax.rem(me - k + n, n)
        pltpu.make_async_remote_copy(
            src_ref=x_ref,
            dst_ref=slots.at[source],
            send_sem=send.at[source],
            recv_sem=recv.at[source],
            device_id=peer(source),
            device_id_type=pl.DeviceIdType.MESH,
        ).wait_recv()
    for copy in copies:
        copy.wait_send()
    acc = slots[0]
    for j in range(1, n):
        acc = acc + slots[j]
    o_ref[...] = acc


def group_sum(tile, axis, collective_id):
    n = lax.axis_size(axis)
    return pl.pallas_call(
        functools.partial(group_sum_kernel, axis),
        out_shape=jax.ShapeDtypeStruct(tile.shape, tile.dtype),
        in_specs=[pl.BlockSpec(memory_space=pltpu.VMEM)],
        out_specs=pl.BlockSpec(memory_space=pltpu.VMEM),
        scratch_shapes=[
            pltpu.VMEM((n,) + tile.shape, tile.dtype),
            pltpu.SemaphoreType.DMA((n,)),
            pltpu.SemaphoreType.DMA((n,)),
        ],
        compiler_params=pltpu.CompilerParams(collective_id=collective_id, has_side_effects=True),
    )(tile)


def total(values):
    tile = jnp.zeros((8, 128), jnp.float32) + jnp.stack(values + [values[0]] * (8 - len(values)))[:, None]
    tile = group_sum(group_sum(tile, "space", 0), "tm", 1)
    return [tile[i, 0] for i in range(len(values))]


def shards(coefficients, counts, coords, pattern, temporal_taps):
    weights = lax.optimization_barrier(spatial_weights(coords, pattern))

    def spread(field):
        return block_product(band_product(field, temporal_taps), weights, pattern)

    banded = band_product(coefficients, temporal_taps, tm_halo)
    moved = to_days(jnp.stack([coefficients, counts.astype(jnp.float32), banded]))
    coef, cnt = moved[0], moved[1]
    latent = block_product(moved[2], weights, pattern)
    intensity = jnp.exp(latent)
    gradient = coef + spread(intensity - cnt)
    residual = -gradient
    direction = residual
    image = spread(direction)
    curved = direction + spread(intensity * image)
    norm_now, curvature, curved_sq = total(
        [jnp.sum(residual * residual), jnp.sum(direction * curved), jnp.sum(curved * curved)]
    )
    step_size = norm_now / curvature
    newton_step = step_size * direction
    residual = residual - step_size * curved
    norm_next = step_size * step_size * curved_sq - norm_now
    direction = residual + norm_next / norm_now * direction
    norm_now = norm_next
    image = spread(direction)
    curved = direction + spread(intensity * image)
    (curvature,) = total([jnp.sum(direction * curved)])
    step_size = norm_now / curvature
    newton_step = newton_step + step_size * direction
    residual = residual - step_size * curved
    out = to_cells(jnp.stack([newton_step, residual]))
    return (out[0], out[1])


def solution(mesh):
    placed = (P("tm", "space"), P("tm", "space"), P(), P(), P())
    return jax.shard_map(
        shards,
        mesh=mesh,
        in_specs=placed,
        out_specs=(P("tm", "space"), P("tm", "space")),
        check_vma=False,
    )
```

```python
import functools

import jax
import jax.numpy as jnp
from jax import lax
from jax.experimental import pallas as pl
from jax.experimental.pallas import tpu as pltpu
from jax.sharding import PartitionSpec as P

BLOCK = 128
BW = 8


support = 0.25
amplitude = 0.2


def wendland(distance):
    scaled = distance / support
    remain = jnp.maximum(1.0 - scaled, 0.0)
    return amplitude * remain**4 * (1.0 + 4.0 * scaled)


def spatial_weights(coords, pattern):
    blocks = pattern.shape[0]
    located = coords.reshape(2, blocks, BLOCK)
    row_coords = located[:, :, None, None, :]
    col_coords = located[:, pattern][:, :, :, :, None]
    delta_x = row_coords[0] - col_coords[0]
    delta_y = row_coords[1] - col_coords[1]
    weight = wendland(jnp.sqrt(delta_x * delta_x + delta_y * delta_y))
    return weight.reshape(blocks, pattern.shape[1] * BLOCK, BLOCK)


def day_order_halo(field):
    spaces, times = lax.axis_size("space"), lax.axis_size("tm")
    place = [snake(spaces, rank // spaces % 2 == 1)[rank % spaces] * times + rank // spaces for rank in range(spaces * times)]
    forward = [(place[i], place[i + 1]) for i in range(len(place) - 1)]
    backward = [(place[i + 1], place[i]) for i in range(len(place) - 1)]
    axes = ("space", "tm")
    low = lax.ppermute(field[field.shape[0] - BW :], axes, forward)
    high = lax.ppermute(field[:BW], axes, backward)
    return jnp.concatenate([low, field, high], axis=0)


def tm_halo(field):
    count = lax.axis_size("tm")
    forward = [(i, i + 1) for i in range(count - 1)]
    backward = [(i + 1, i) for i in range(count - 1)]
    low = lax.ppermute(field[field.shape[0] - BW :], "tm", forward)
    high = lax.ppermute(field[:BW], "tm", backward)
    return jnp.concatenate([low, field, high], axis=0)


def band_product(field, temporal_taps, halo=None):
    length = field.shape[0]
    padded = (halo or day_order_halo)(field)
    summed = temporal_taps[0] * field
    for offset in range(1, BW + 1):
        summed = summed + temporal_taps[offset] * (
            padded[BW - offset : BW - offset + length] + padded[BW + offset : BW + offset + length]
        )
    return summed


def block_product(field, weights, pattern):
    day_count = field.shape[0]
    blocks = pattern.shape[0]
    blocked = field.reshape(day_count, blocks, BLOCK)
    picked = blocked[:, pattern].reshape(day_count, blocks, pattern.shape[1] * BLOCK)
    out = jnp.einsum("rkc,drk->drc", weights, picked, precision=lax.Precision.HIGH)
    return out.reshape(day_count, blocks * BLOCK)


def snake(spaces, odd):
    half = spaces // 2
    order = [i if i < half else spaces + half - 1 - i for i in range(spaces)]
    return order[::-1] if odd else order


def chain_of(spaces, odd):
    order = snake(spaces, odd)
    return [order.index(i) for i in range(spaces)]


def row_pick(table_even, table_odd):
    odd = lax.rem(lax.axis_index("tm"), 2) == 1
    return jnp.where(odd, jnp.array(table_odd), jnp.array(table_even))


def to_days(field):
    n = lax.axis_size("space")
    k, days, cells = field.shape
    picks = row_pick(chain_of(n, False), chain_of(n, True))
    chunked = field.reshape(k, n, days // n, cells)[:, picks].transpose(1, 0, 2, 3)
    got = lax.all_to_all(chunked, "space", split_axis=0, concat_axis=0, tiled=True)
    return got.transpose(1, 2, 0, 3).reshape(k, days // n, n * cells)


def to_cells(field):
    n = lax.axis_size("space")
    k, days, cells = field.shape
    chunked = field.reshape(k, days, n, cells // n).transpose(2, 0, 1, 3)
    got = lax.all_to_all(chunked, "space", split_axis=0, concat_axis=0, tiled=True)
    picks = row_pick(snake(n, False), snake(n, True))
    return got[picks].transpose(1, 0, 2, 3).reshape(k, n * days, cells // n)


def group_sum_kernel(axis, x_ref, o_ref, slots, send, recv):
    n = slots.shape[0]
    me = lax.axis_index(axis)

    def peer(index):
        return {axis: index}

    barrier = pltpu.get_barrier_semaphore()
    for k in range(1, n):
        pl.semaphore_signal(barrier, 1, device_id=peer(lax.rem(me + k, n)), device_id_type=pl.DeviceIdType.MESH)
    pl.semaphore_wait(barrier, n - 1)
    copies = []
    for k in range(1, n):
        target = lax.rem(me + k, n)
        copy = pltpu.make_async_remote_copy(
            src_ref=x_ref,
            dst_ref=slots.at[me],
            send_sem=send.at[target],
            recv_sem=recv.at[me],
            device_id=peer(target),
            device_id_type=pl.DeviceIdType.MESH,
        )
        copy.start()
        copies.append(copy)
    slots[me] = x_ref[...]
    for k in range(1, n):
        source = lax.rem(me - k + n, n)
        pltpu.make_async_remote_copy(
            src_ref=x_ref,
            dst_ref=slots.at[source],
            send_sem=send.at[source],
            recv_sem=recv.at[source],
            device_id=peer(source),
            device_id_type=pl.DeviceIdType.MESH,
        ).wait_recv()
    for copy in copies:
        copy.wait_send()
    acc = slots[0]
    for j in range(1, n):
        acc = acc + slots[j]
    o_ref[...] = acc


def group_sum(tile, axis, collective_id):
    n = lax.axis_size(axis)
    return pl.pallas_call(
        functools.partial(group_sum_kernel, axis),
        out_shape=jax.ShapeDtypeStruct(tile.shape, tile.dtype),
        in_specs=[pl.BlockSpec(memory_space=pltpu.VMEM)],
        out_specs=pl.BlockSpec(memory_space=pltpu.VMEM),
        scratch_shapes=[
            pltpu.VMEM((n,) + tile.shape, tile.dtype),
            pltpu.SemaphoreType.DMA((n,)),
            pltpu.SemaphoreType.DMA((n,)),
        ],
        compiler_params=pltpu.CompilerParams(collective_id=collective_id, has_side_effects=True),
    )(tile)


def total(values):
    tile = jnp.zeros((8, 128), jnp.float32) + jnp.stack(values + [values[0]] * (8 - len(values)))[:, None]
    tile = group_sum(group_sum(tile, "space", 0), "tm", 1)
    return [tile[i, 0] for i in range(len(values))]


def shards(coefficients, counts, coords, pattern, temporal_taps):
    weights = lax.optimization_barrier(spatial_weights(coords, pattern))

    def spread(field):
        return block_product(band_product(field, temporal_taps), weights, pattern)

    banded = band_product(coefficients, temporal_taps, tm_halo)
    moved = to_days(jnp.stack([coefficients, counts.astype(jnp.float32), banded]))
    coef, cnt = moved[0], moved[1]
    latent = block_product(moved[2], weights, pattern)
    intensity = jnp.exp(latent)
    gradient = coef + spread(intensity - cnt)
    residual = -gradient
    direction = residual
    image = spread(direction)
    curved = direction + spread(intensity * image)
    norm_now, curvature, curved_sq = total(
        [jnp.sum(residual * residual), jnp.sum(direction * curved), jnp.sum(curved * curved)]
    )
    step_size = norm_now / curvature
    newton_step = step_size * direction
    residual = residual - step_size * curved
    norm_next = step_size * step_size * curved_sq - norm_now
    direction = residual + norm_next / norm_now * direction
    norm_now = norm_next
    image = spread(direction)
    curved = direction + spread(intensity * image)
    (curvature,) = total([jnp.sum(direction * curved)])
    step_size = norm_now / curvature
    newton_step = newton_step + step_size * direction
    residual = residual - step_size * curved
    out = to_cells(jnp.stack([newton_step, residual]))
    return (out[0], out[1])


def solution(mesh):
    placed = (P("tm", "space"), P("tm", "space"), P(), P(), P())
    return jax.shard_map(
        shards,
        mesh=mesh,
        in_specs=placed,
        out_specs=(P("tm", "space"), P("tm", "space")),
        check_vma=False,
    )
```

```python
import functools

import jax
import jax.numpy as jnp
from jax import lax
from jax.experimental import pallas as pl
from jax.experimental.pallas import tpu as pltpu
from jax.sharding import PartitionSpec as P

BLOCK = 128
BW = 8


support = 0.25
amplitude = 0.2


def wendland(distance):
    scaled = distance / support
    remain = jnp.maximum(1.0 - scaled, 0.0)
    return amplitude * remain**4 * (1.0 + 4.0 * scaled)


def spatial_weights(coords, pattern):
    blocks = pattern.shape[0]
    located = coords.reshape(2, blocks, BLOCK)
    row_coords = located[:, :, None, None, :]
    col_coords = located[:, pattern][:, :, :, :, None]
    delta_x = row_coords[0] - col_coords[0]
    delta_y = row_coords[1] - col_coords[1]
    weight = wendland(jnp.sqrt(delta_x * delta_x + delta_y * delta_y))
    return weight.reshape(blocks, pattern.shape[1] * BLOCK, BLOCK)


def day_order_halo(field):
    spaces, times = lax.axis_size("space"), lax.axis_size("tm")
    order = snake(spaces)
    place = [order[rank % spaces] * times + rank // spaces for rank in range(spaces * times)]
    forward = [(place[i], place[i + 1]) for i in range(len(place) - 1)]
    backward = [(place[i + 1], place[i]) for i in range(len(place) - 1)]
    axes = ("space", "tm")
    low = lax.ppermute(field[:, field.shape[1] - BW :], axes, forward)
    high = lax.ppermute(field[:, :BW], axes, backward)
    return jnp.concatenate([low, field, high], axis=1)


def tm_halo(field):
    count = lax.axis_size("tm")
    forward = [(i, i + 1) for i in range(count - 1)]
    backward = [(i + 1, i) for i in range(count - 1)]
    low = lax.ppermute(field[field.shape[0] - BW :], "tm", forward)
    high = lax.ppermute(field[:BW], "tm", backward)
    return jnp.concatenate([low, field, high], axis=0)


def band_product(field, temporal_taps, halo=None, axis=1):
    length = field.shape[axis]
    padded = (halo or day_order_halo)(field)

    def days(start):
        return lax.slice_in_dim(padded, start, start + length, axis=axis)

    summed = temporal_taps[0] * field
    for offset in range(1, BW + 1):
        summed = summed + temporal_taps[offset] * (days(BW - offset) + days(BW + offset))
    return summed


def block_product(field, weights, pattern):
    blocks, day_count, _ = field.shape
    picked = field[pattern].transpose(0, 2, 1, 3).reshape(blocks, day_count, pattern.shape[1] * BLOCK)
    return jnp.einsum("rkc,rdk->rdc", weights, picked, precision=lax.Precision.HIGH)


def snake(spaces):
    half = spaces // 2
    return [i if i < half else spaces + half - 1 - i for i in range(spaces)]


def to_days(field):
    n = lax.axis_size("space")
    k, days, cells = field.shape
    chunked = field.reshape(k, n, days // n, cells)[:, jnp.array(snake(n))].transpose(1, 0, 2, 3)
    got = lax.all_to_all(chunked, "space", split_axis=0, concat_axis=0, tiled=True)
    got = got.reshape(n, k, days // n, cells // BLOCK, BLOCK).transpose(1, 0, 3, 2, 4)
    return got.reshape(k, n * cells // BLOCK, days // n, BLOCK)


def to_cells(field):
    n = lax.axis_size("space")
    k, blocks, days, _ = field.shape
    cells = blocks * BLOCK
    chunked = field.reshape(k, n, blocks // n, days, BLOCK).transpose(1, 0, 3, 2, 4)
    chunked = chunked.reshape(n, k, days, cells // n)
    got = lax.all_to_all(chunked, "space", split_axis=0, concat_axis=0, tiled=True)
    return got[jnp.array(snake(n))].transpose(1, 0, 2, 3).reshape(k, n * days, cells // n)


def group_sum_kernel(axis, x_ref, o_ref, slots, send, recv):
    n = slots.shape[0]
    me = lax.axis_index(axis)

    def peer(index):
        return {axis: index}

    barrier = pltpu.get_barrier_semaphore()
    for k in range(1, n):
        pl.semaphore_signal(barrier, 1, device_id=peer(lax.rem(me + k, n)), device_id_type=pl.DeviceIdType.MESH)
    pl.semaphore_wait(barrier, n - 1)
    copies = []
    for k in range(1, n):
        target = lax.rem(me + k, n)
        copy = pltpu.make_async_remote_copy(
            src_ref=x_ref,
            dst_ref=slots.at[me],
            send_sem=send.at[target],
            recv_sem=recv.at[me],
            device_id=peer(target),
            device_id_type=pl.DeviceIdType.MESH,
        )
        copy.start()
        copies.append(copy)
    slots[me] = x_ref[...]
    for k in range(1, n):
        source = lax.rem(me - k + n, n)
        pltpu.make_async_remote_copy(
            src_ref=x_ref,
            dst_ref=slots.at[source],
            send_sem=send.at[source],
            recv_sem=recv.at[source],
            device_id=peer(source),
            device_id_type=pl.DeviceIdType.MESH,
        ).wait_recv()
    for copy in copies:
        copy.wait_send()
    acc = slots[0]
    for j in range(1, n):
        acc = acc + slots[j]
    o_ref[...] = acc


def group_sum(tile, axis, collective_id):
    n = lax.axis_size(axis)
    return pl.pallas_call(
        functools.partial(group_sum_kernel, axis),
        out_shape=jax.ShapeDtypeStruct(tile.shape, tile.dtype),
        in_specs=[pl.BlockSpec(memory_space=pltpu.VMEM)],
        out_specs=pl.BlockSpec(memory_space=pltpu.VMEM),
        scratch_shapes=[
            pltpu.VMEM((n,) + tile.shape, tile.dtype),
            pltpu.SemaphoreType.DMA((n,)),
            pltpu.SemaphoreType.DMA((n,)),
        ],
        compiler_params=pltpu.CompilerParams(collective_id=collective_id, has_side_effects=True),
    )(tile)


def total(values):
    tile = jnp.zeros((8, 128), jnp.float32) + jnp.stack(values + [values[0]] * (8 - len(values)))[:, None]
    tile = group_sum(group_sum(tile, "space", 0), "tm", 1)
    return [tile[i, 0] for i in range(len(values))]


def shards(coefficients, counts, coords, pattern, temporal_taps):
    weights = lax.optimization_barrier(spatial_weights(coords, pattern))

    def spread(field):
        return block_product(band_product(field, temporal_taps), weights, pattern)

    banded = band_product(coefficients, temporal_taps, tm_halo, axis=0)
    moved = to_days(jnp.stack([coefficients, counts.astype(jnp.float32), banded]))
    coef, cnt = moved[0], moved[1]
    latent = block_product(moved[2], weights, pattern)
    intensity = jnp.exp(latent)
    gradient = coef + spread(intensity - cnt)
    residual = -gradient
    direction = residual
    image = spread(direction)
    curved = direction + spread(intensity * image)
    norm_now, curvature, curved_sq = total(
        [jnp.sum(residual * residual), jnp.sum(direction * curved), jnp.sum(curved * curved)]
    )
    step_size = norm_now / curvature
    newton_step = step_size * direction
    residual = residual - step_size * curved
    norm_next = step_size * step_size * curved_sq - norm_now
    direction = residual + norm_next / norm_now * direction
    norm_now = norm_next
    image = spread(direction)
    curved = direction + spread(intensity * image)
    (curvature,) = total([jnp.sum(direction * curved)])
    step_size = norm_now / curvature
    newton_step = newton_step + step_size * direction
    residual = residual - step_size * curved
    out = to_cells(jnp.stack([newton_step, residual]))
    return (out[0], out[1])


def solution(mesh):
    placed = (P("tm", "space"), P("tm", "space"), P(), P(), P())
    return jax.shard_map(
        shards,
        mesh=mesh,
        in_specs=placed,
        out_specs=(P("tm", "space"), P("tm", "space")),
        check_vma=False,
    )
```

```python
import functools

import jax
import jax.numpy as jnp
from jax import lax
from jax.experimental import pallas as pl
from jax.experimental.pallas import tpu as pltpu
from jax.sharding import PartitionSpec as P

BLOCK = 128
BW = 8


support = 0.25
amplitude = 0.2


def wendland(distance):
    scaled = distance / support
    remain = jnp.maximum(1.0 - scaled, 0.0)
    return amplitude * remain**4 * (1.0 + 4.0 * scaled)


def spatial_weights(coords, pattern):
    blocks = pattern.shape[0]
    located = coords.reshape(2, blocks, BLOCK)
    row_coords = located[:, :, None, None, :]
    col_coords = located[:, pattern][:, :, :, :, None]
    delta_x = row_coords[0] - col_coords[0]
    delta_y = row_coords[1] - col_coords[1]
    weight = wendland(jnp.sqrt(delta_x * delta_x + delta_y * delta_y))
    return weight.reshape(blocks, pattern.shape[1] * BLOCK, BLOCK)


def day_order_halo(field):
    spaces, times = lax.axis_size("space"), lax.axis_size("tm")
    order = snake(spaces)
    place = [order[rank % spaces] * times + rank // spaces for rank in range(spaces * times)]
    forward = [(place[i], place[i + 1]) for i in range(len(place) - 1)]
    backward = [(place[i + 1], place[i]) for i in range(len(place) - 1)]
    axes = ("space", "tm")
    low = lax.ppermute(field[:, field.shape[1] - BW :], axes, forward)
    high = lax.ppermute(field[:, :BW], axes, backward)
    return jnp.concatenate([low, field, high], axis=1)


def tm_halo(field):
    count = lax.axis_size("tm")
    forward = [(i, i + 1) for i in range(count - 1)]
    backward = [(i + 1, i) for i in range(count - 1)]
    low = lax.ppermute(field[field.shape[0] - BW :], "tm", forward)
    high = lax.ppermute(field[:BW], "tm", backward)
    return jnp.concatenate([low, field, high], axis=0)


def band_product(field, temporal_taps, halo=None, axis=1):
    length = field.shape[axis]
    padded = (halo or day_order_halo)(field)

    def days(start):
        return lax.slice_in_dim(padded, start, start + length, axis=axis)

    summed = temporal_taps[0] * field
    for offset in range(1, BW + 1):
        summed = summed + temporal_taps[offset] * (days(BW - offset) + days(BW + offset))
    return summed


def block_product(field, weights, pattern):
    blocks, day_count, _ = field.shape
    picked = field[pattern].transpose(0, 2, 1, 3).reshape(blocks, day_count, pattern.shape[1] * BLOCK)
    return jnp.einsum("rkc,rdk->rdc", weights, picked, precision=lax.Precision.HIGH)


def snake(spaces):
    half = spaces // 2
    return [i if i < half else spaces + half - 1 - i for i in range(spaces)]


def to_days(field):
    n = lax.axis_size("space")
    k, days, cells = field.shape
    chunked = field.reshape(k, n, days // n, cells)[:, jnp.array(snake(n))].transpose(1, 0, 2, 3)
    got = lax.all_to_all(chunked, "space", split_axis=0, concat_axis=0, tiled=True)
    got = got.reshape(n, k, days // n, cells // BLOCK, BLOCK).transpose(1, 0, 3, 2, 4)
    return got.reshape(k, n * cells // BLOCK, days // n, BLOCK)


def to_cells(field):
    n = lax.axis_size("space")
    k, blocks, days, _ = field.shape
    cells = blocks * BLOCK
    chunked = field.reshape(k, n, blocks // n, days, BLOCK).transpose(1, 0, 3, 2, 4)
    chunked = chunked.reshape(n, k, days, cells // n)
    got = lax.all_to_all(chunked, "space", split_axis=0, concat_axis=0, tiled=True)
    return got[jnp.array(snake(n))].transpose(1, 0, 2, 3).reshape(k, n * days, cells // n)


def group_sum_kernel(axis, x_ref, o_ref, slots, send, recv):
    n = slots.shape[0]
    me = lax.axis_index(axis)

    def peer(index):
        return {axis: index}

    barrier = pltpu.get_barrier_semaphore()
    for k in range(1, n):
        pl.semaphore_signal(barrier, 1, device_id=peer(lax.rem(me + k, n)), device_id_type=pl.DeviceIdType.MESH)
    pl.semaphore_wait(barrier, n - 1)
    copies = []
    for k in range(1, n):
        target = lax.rem(me + k, n)
        copy = pltpu.make_async_remote_copy(
            src_ref=x_ref,
            dst_ref=slots.at[me],
            send_sem=send.at[target],
            recv_sem=recv.at[me],
            device_id=peer(target),
            device_id_type=pl.DeviceIdType.MESH,
        )
        copy.start()
        copies.append(copy)
    slots[me] = x_ref[...]
    for k in range(1, n):
        source = lax.rem(me - k + n, n)
        pltpu.make_async_remote_copy(
            src_ref=x_ref,
            dst_ref=slots.at[source],
            send_sem=send.at[source],
            recv_sem=recv.at[source],
            device_id=peer(source),
            device_id_type=pl.DeviceIdType.MESH,
        ).wait_recv()
    for copy in copies:
        copy.wait_send()
    acc = slots[0]
    for j in range(1, n):
        acc = acc + slots[j]
    o_ref[...] = acc


def group_sum(tile, axis, collective_id):
    n = lax.axis_size(axis)
    return pl.pallas_call(
        functools.partial(group_sum_kernel, axis),
        out_shape=jax.ShapeDtypeStruct(tile.shape, tile.dtype),
        in_specs=[pl.BlockSpec(memory_space=pltpu.VMEM)],
        out_specs=pl.BlockSpec(memory_space=pltpu.VMEM),
        scratch_shapes=[
            pltpu.VMEM((n,) + tile.shape, tile.dtype),
            pltpu.SemaphoreType.DMA((n,)),
            pltpu.SemaphoreType.DMA((n,)),
        ],
        compiler_params=pltpu.CompilerParams(collective_id=collective_id, has_side_effects=True),
    )(tile)


def total(products):
    count = len(products)
    lanes = jnp.stack(products).reshape(count, -1, 128).sum(axis=1)
    tile = jnp.pad(lanes, ((0, 8 - count), (0, 0)))
    tile = group_sum(group_sum(tile, "space", 0), "tm", 1)
    return [jnp.sum(tile[i]) for i in range(count)]


def shards(coefficients, counts, coords, pattern, temporal_taps):
    weights = lax.optimization_barrier(spatial_weights(coords, pattern))

    def spread(field):
        return block_product(band_product(field, temporal_taps), weights, pattern)

    banded = band_product(coefficients, temporal_taps, tm_halo, axis=0)
    moved = to_days(jnp.stack([coefficients, counts.astype(jnp.float32), banded]))
    coef, cnt = moved[0], moved[1]
    latent = block_product(moved[2], weights, pattern)
    intensity = jnp.exp(latent)
    gradient = coef + spread(intensity - cnt)
    residual = -gradient
    direction = residual
    image = spread(direction)
    curved = direction + spread(intensity * image)
    norm_now, curvature, curved_sq = total([residual * residual, direction * curved, curved * curved])
    step_size = norm_now / curvature
    newton_step = step_size * direction
    residual = residual - step_size * curved
    norm_next = step_size * step_size * curved_sq - norm_now
    direction = residual + norm_next / norm_now * direction
    norm_now = norm_next
    image = spread(direction)
    curved = direction + spread(intensity * image)
    (curvature,) = total([direction * curved])
    step_size = norm_now / curvature
    newton_step = newton_step + step_size * direction
    residual = residual - step_size * curved
    out = to_cells(jnp.stack([newton_step, residual]))
    return (out[0], out[1])


def solution(mesh):
    placed = (P("tm", "space"), P("tm", "space"), P(), P(), P())
    return jax.shard_map(
        shards,
        mesh=mesh,
        in_specs=placed,
        out_specs=(P("tm", "space"), P("tm", "space")),
        check_vma=False,
    )
```

```python
import functools

import jax
import jax.numpy as jnp
from jax import lax
from jax.experimental import pallas as pl
from jax.experimental.pallas import tpu as pltpu
from jax.sharding import PartitionSpec as P

BLOCK = 128
BW = 8


support = 0.25
amplitude = 0.2


def wendland(distance):
    scaled = distance / support
    remain = jnp.maximum(1.0 - scaled, 0.0)
    return amplitude * remain**4 * (1.0 + 4.0 * scaled)


def spatial_weights(coords, pattern):
    blocks = pattern.shape[0]
    located = coords.reshape(2, blocks, BLOCK)
    row_coords = located[:, :, None, None, :]
    col_coords = located[:, pattern][:, :, :, :, None]
    delta_x = row_coords[0] - col_coords[0]
    delta_y = row_coords[1] - col_coords[1]
    weight = wendland(jnp.sqrt(delta_x * delta_x + delta_y * delta_y))
    return weight.reshape(blocks, pattern.shape[1] * BLOCK, BLOCK)


def day_order_halo(field):
    spaces, times = lax.axis_size("space"), lax.axis_size("tm")
    order = snake(spaces)
    place = [order[rank % spaces] * times + rank // spaces for rank in range(spaces * times)]
    forward = [(place[i], place[i + 1]) for i in range(len(place) - 1)]
    backward = [(place[i + 1], place[i]) for i in range(len(place) - 1)]
    axes = ("space", "tm")
    low = lax.ppermute(field[:, field.shape[1] - BW :], axes, forward)
    high = lax.ppermute(field[:, :BW], axes, backward)
    return jnp.concatenate([low, field, high], axis=1)


def tm_halo(field):
    count = lax.axis_size("tm")
    forward = [(i, i + 1) for i in range(count - 1)]
    backward = [(i + 1, i) for i in range(count - 1)]
    low = lax.ppermute(field[field.shape[0] - BW :], "tm", forward)
    high = lax.ppermute(field[:BW], "tm", backward)
    return jnp.concatenate([low, field, high], axis=0)


def band_product(field, temporal_taps, halo=None, axis=1):
    length = field.shape[axis]
    padded = (halo or day_order_halo)(field)

    def days(start):
        return lax.slice_in_dim(padded, start, start + length, axis=axis)

    if axis == 0:
        summed = temporal_taps[0] * field
        for offset in range(1, BW + 1):
            summed = summed + temporal_taps[offset] * (days(BW - offset) + days(BW + offset))
        return summed
    lag = jnp.arange(length + 2 * BW)[None, :] - jnp.arange(length)[:, None] - BW
    band = jnp.where(jnp.abs(lag) <= BW, temporal_taps[jnp.clip(jnp.abs(lag), 0, BW)], 0.0)
    return jnp.einsum("de,rec->rdc", band, padded, precision=lax.Precision.HIGHEST)


def block_product(field, weights, pattern):
    blocks, day_count, _ = field.shape
    picked = field[pattern].transpose(0, 2, 1, 3).reshape(blocks, day_count, pattern.shape[1] * BLOCK)
    return jnp.einsum("rkc,rdk->rdc", weights, picked, precision=lax.Precision.HIGH)


def snake(spaces):
    half = spaces // 2
    return [i if i < half else spaces + half - 1 - i for i in range(spaces)]


def to_days(field):
    n = lax.axis_size("space")
    k, days, cells = field.shape
    chunked = field.reshape(k, n, days // n, cells)[:, jnp.array(snake(n))].transpose(1, 0, 2, 3)
    got = lax.all_to_all(chunked, "space", split_axis=0, concat_axis=0, tiled=True)
    got = got.reshape(n, k, days // n, cells // BLOCK, BLOCK).transpose(1, 0, 3, 2, 4)
    return got.reshape(k, n * cells // BLOCK, days // n, BLOCK)


def to_cells(field):
    n = lax.axis_size("space")
    k, blocks, days, _ = field.shape
    cells = blocks * BLOCK
    chunked = field.reshape(k, n, blocks // n, days, BLOCK).transpose(1, 0, 3, 2, 4)
    chunked = chunked.reshape(n, k, days, cells // n)
    got = lax.all_to_all(chunked, "space", split_axis=0, concat_axis=0, tiled=True)
    return got[jnp.array(snake(n))].transpose(1, 0, 2, 3).reshape(k, n * days, cells // n)


def group_sum_kernel(axis, x_ref, o_ref, slots, send, recv):
    n = slots.shape[0]
    me = lax.axis_index(axis)

    def peer(index):
        return {axis: index}

    barrier = pltpu.get_barrier_semaphore()
    for k in range(1, n):
        pl.semaphore_signal(barrier, 1, device_id=peer(lax.rem(me + k, n)), device_id_type=pl.DeviceIdType.MESH)
    pl.semaphore_wait(barrier, n - 1)
    copies = []
    for k in range(1, n):
        target = lax.rem(me + k, n)
        copy = pltpu.make_async_remote_copy(
            src_ref=x_ref,
            dst_ref=slots.at[me],
            send_sem=send.at[target],
            recv_sem=recv.at[me],
            device_id=peer(target),
            device_id_type=pl.DeviceIdType.MESH,
        )
        copy.start()
        copies.append(copy)
    slots[me] = x_ref[...]
    for k in range(1, n):
        source = lax.rem(me - k + n, n)
        pltpu.make_async_remote_copy(
            src_ref=x_ref,
            dst_ref=slots.at[source],
            send_sem=send.at[source],
            recv_sem=recv.at[source],
            device_id=peer(source),
            device_id_type=pl.DeviceIdType.MESH,
        ).wait_recv()
    for copy in copies:
        copy.wait_send()
    acc = slots[0]
    for j in range(1, n):
        acc = acc + slots[j]
    o_ref[...] = acc


def group_sum(tile, axis, collective_id):
    n = lax.axis_size(axis)
    return pl.pallas_call(
        functools.partial(group_sum_kernel, axis),
        out_shape=jax.ShapeDtypeStruct(tile.shape, tile.dtype),
        in_specs=[pl.BlockSpec(memory_space=pltpu.VMEM)],
        out_specs=pl.BlockSpec(memory_space=pltpu.VMEM),
        scratch_shapes=[
            pltpu.VMEM((n,) + tile.shape, tile.dtype),
            pltpu.SemaphoreType.DMA((n,)),
            pltpu.SemaphoreType.DMA((n,)),
        ],
        compiler_params=pltpu.CompilerParams(collective_id=collective_id, has_side_effects=True),
    )(tile)


def total(products):
    count = len(products)
    lanes = jnp.stack(products).reshape(count, -1, 128).sum(axis=1)
    tile = jnp.pad(lanes, ((0, 8 - count), (0, 0)))
    tile = group_sum(group_sum(tile, "space", 0), "tm", 1)
    return [jnp.sum(tile[i]) for i in range(count)]


def shards(coefficients, counts, coords, pattern, temporal_taps):
    weights = lax.optimization_barrier(spatial_weights(coords, pattern))

    def spread(field):
        return block_product(band_product(field, temporal_taps), weights, pattern)

    banded = band_product(coefficients, temporal_taps, tm_halo, axis=0)
    moved = to_days(jnp.stack([coefficients, counts.astype(jnp.float32), banded]))
    coef, cnt = moved[0], moved[1]
    latent = block_product(moved[2], weights, pattern)
    intensity = jnp.exp(latent)
    gradient = coef + spread(intensity - cnt)
    residual = -gradient
    direction = residual
    image = spread(direction)
    curved = direction + spread(intensity * image)
    norm_now, curvature, curved_sq = total([residual * residual, direction * curved, curved * curved])
    step_size = norm_now / curvature
    newton_step = step_size * direction
    residual = residual - step_size * curved
    norm_next = step_size * step_size * curved_sq - norm_now
    direction = residual + norm_next / norm_now * direction
    norm_now = norm_next
    image = spread(direction)
    curved = direction + spread(intensity * image)
    (curvature,) = total([direction * curved])
    step_size = norm_now / curvature
    newton_step = newton_step + step_size * direction
    residual = residual - step_size * curved
    out = to_cells(jnp.stack([newton_step, residual]))
    return (out[0], out[1])


def solution(mesh):
    placed = (P("tm", "space"), P("tm", "space"), P(), P(), P())
    return jax.shard_map(
        shards,
        mesh=mesh,
        in_specs=placed,
        out_specs=(P("tm", "space"), P("tm", "space")),
        check_vma=False,
    )
```

```python
import functools

import jax
import jax.numpy as jnp
from jax import lax
from jax.experimental import pallas as pl
from jax.experimental.pallas import tpu as pltpu
from jax.sharding import PartitionSpec as P

BLOCK = 128
BW = 8


support = 0.25
amplitude = 0.2


def wendland(distance):
    scaled = distance / support
    remain = jnp.maximum(1.0 - scaled, 0.0)
    return amplitude * remain**4 * (1.0 + 4.0 * scaled)


def spatial_weights(coords, pattern):
    blocks = pattern.shape[0]
    located = coords.reshape(2, blocks, BLOCK)
    row_coords = located[:, :, None, None, :]
    col_coords = located[:, pattern][:, :, :, :, None]
    delta_x = row_coords[0] - col_coords[0]
    delta_y = row_coords[1] - col_coords[1]
    weight = wendland(jnp.sqrt(delta_x * delta_x + delta_y * delta_y))
    return weight.reshape(blocks, pattern.shape[1] * BLOCK, BLOCK)


def day_order_halo(field):
    spaces, times = lax.axis_size("space"), lax.axis_size("tm")
    order = snake(spaces)
    place = [order[rank % spaces] * times + rank // spaces for rank in range(spaces * times)]
    forward = [(place[i], place[i + 1]) for i in range(len(place) - 1)]
    backward = [(place[i + 1], place[i]) for i in range(len(place) - 1)]
    axes = ("space", "tm")
    low = lax.ppermute(field[:, field.shape[1] - BW :], axes, forward)
    high = lax.ppermute(field[:, :BW], axes, backward)
    return jnp.concatenate([low, field, high], axis=1)


def tm_halo(field):
    count = lax.axis_size("tm")
    forward = [(i, i + 1) for i in range(count - 1)]
    backward = [(i + 1, i) for i in range(count - 1)]
    low = lax.ppermute(field[field.shape[0] - BW :], "tm", forward)
    high = lax.ppermute(field[:BW], "tm", backward)
    return jnp.concatenate([low, field, high], axis=0)


def band_product(field, temporal_taps, halo=None, axis=1):
    length = field.shape[axis]
    padded = (halo or day_order_halo)(field)

    def days(start):
        return lax.slice_in_dim(padded, start, start + length, axis=axis)

    lag = jnp.arange(length + 2 * BW)[None, :] - jnp.arange(length)[:, None] - BW
    band = jnp.where(jnp.abs(lag) <= BW, temporal_taps[jnp.clip(jnp.abs(lag), 0, BW)], 0.0)
    if axis == 0:
        return jnp.einsum("de,ec->dc", band, padded, precision=lax.Precision.HIGHEST)
    return jnp.einsum("de,rec->rdc", band, padded, precision=lax.Precision.HIGHEST)


def block_product(field, weights, pattern):
    blocks, day_count, _ = field.shape
    picked = field[pattern].transpose(0, 2, 1, 3).reshape(blocks, day_count, pattern.shape[1] * BLOCK)
    return jnp.einsum("rkc,rdk->rdc", weights, picked, precision=lax.Precision.HIGH)


def snake(spaces):
    half = spaces // 2
    return [i if i < half else spaces + half - 1 - i for i in range(spaces)]


def to_days(field):
    n = lax.axis_size("space")
    k, days, cells = field.shape
    chunked = field.reshape(k, n, days // n, cells)[:, jnp.array(snake(n))].transpose(1, 0, 2, 3)
    got = lax.all_to_all(chunked, "space", split_axis=0, concat_axis=0, tiled=True)
    got = got.reshape(n, k, days // n, cells // BLOCK, BLOCK).transpose(1, 0, 3, 2, 4)
    return got.reshape(k, n * cells // BLOCK, days // n, BLOCK)


def to_cells(field):
    n = lax.axis_size("space")
    k, blocks, days, _ = field.shape
    cells = blocks * BLOCK
    chunked = field.reshape(k, n, blocks // n, days, BLOCK).transpose(1, 0, 3, 2, 4)
    chunked = chunked.reshape(n, k, days, cells // n)
    got = lax.all_to_all(chunked, "space", split_axis=0, concat_axis=0, tiled=True)
    return got[jnp.array(snake(n))].transpose(1, 0, 2, 3).reshape(k, n * days, cells // n)


def group_sum_kernel(axis, x_ref, o_ref, slots, send, recv):
    n = slots.shape[0]
    me = lax.axis_index(axis)

    def peer(index):
        return {axis: index}

    barrier = pltpu.get_barrier_semaphore()
    for k in range(1, n):
        pl.semaphore_signal(barrier, 1, device_id=peer(lax.rem(me + k, n)), device_id_type=pl.DeviceIdType.MESH)
    pl.semaphore_wait(barrier, n - 1)
    copies = []
    for k in range(1, n):
        target = lax.rem(me + k, n)
        copy = pltpu.make_async_remote_copy(
            src_ref=x_ref,
            dst_ref=slots.at[me],
            send_sem=send.at[target],
            recv_sem=recv.at[me],
            device_id=peer(target),
            device_id_type=pl.DeviceIdType.MESH,
        )
        copy.start()
        copies.append(copy)
    slots[me] = x_ref[...]
    for k in range(1, n):
        source = lax.rem(me - k + n, n)
        pltpu.make_async_remote_copy(
            src_ref=x_ref,
            dst_ref=slots.at[source],
            send_sem=send.at[source],
            recv_sem=recv.at[source],
            device_id=peer(source),
            device_id_type=pl.DeviceIdType.MESH,
        ).wait_recv()
    for copy in copies:
        copy.wait_send()
    acc = slots[0]
    for j in range(1, n):
        acc = acc + slots[j]
    o_ref[...] = acc


def group_sum(tile, axis, collective_id):
    n = lax.axis_size(axis)
    return pl.pallas_call(
        functools.partial(group_sum_kernel, axis),
        out_shape=jax.ShapeDtypeStruct(tile.shape, tile.dtype),
        in_specs=[pl.BlockSpec(memory_space=pltpu.VMEM)],
        out_specs=pl.BlockSpec(memory_space=pltpu.VMEM),
        scratch_shapes=[
            pltpu.VMEM((n,) + tile.shape, tile.dtype),
            pltpu.SemaphoreType.DMA((n,)),
            pltpu.SemaphoreType.DMA((n,)),
        ],
        compiler_params=pltpu.CompilerParams(collective_id=collective_id, has_side_effects=True),
    )(tile)


def total(products):
    count = len(products)
    lanes = jnp.stack(products).reshape(count, -1, 128).sum(axis=1)
    tile = jnp.pad(lanes, ((0, 8 - count), (0, 0)))
    tile = group_sum(group_sum(tile, "space", 0), "tm", 1)
    return [jnp.sum(tile[i]) for i in range(count)]


def shards(coefficients, counts, coords, pattern, temporal_taps):
    weights = lax.optimization_barrier(spatial_weights(coords, pattern))

    def spread(field):
        return block_product(band_product(field, temporal_taps), weights, pattern)

    banded = band_product(coefficients, temporal_taps, tm_halo, axis=0)
    moved = to_days(jnp.stack([coefficients, counts.astype(jnp.float32), banded]))
    coef, cnt = moved[0], moved[1]
    latent = block_product(moved[2], weights, pattern)
    intensity = jnp.exp(latent)
    gradient = coef + spread(intensity - cnt)
    residual = -gradient
    direction = residual
    image = spread(direction)
    curved = direction + spread(intensity * image)
    norm_now, curvature, curved_sq = total([residual * residual, direction * curved, curved * curved])
    step_size = norm_now / curvature
    newton_step = step_size * direction
    residual = residual - step_size * curved
    norm_next = step_size * step_size * curved_sq - norm_now
    direction = residual + norm_next / norm_now * direction
    norm_now = norm_next
    image = spread(direction)
    curved = direction + spread(intensity * image)
    (curvature,) = total([direction * curved])
    step_size = norm_now / curvature
    newton_step = newton_step + step_size * direction
    residual = residual - step_size * curved
    out = to_cells(jnp.stack([newton_step, residual]))
    return (out[0], out[1])


def solution(mesh):
    placed = (P("tm", "space"), P("tm", "space"), P(), P(), P())
    return jax.shard_map(
        shards,
        mesh=mesh,
        in_specs=placed,
        out_specs=(P("tm", "space"), P("tm", "space")),
        check_vma=False,
    )
```
